128 devices in a mesh: section: 2 (over core), dp: 16 (over y, x), mp: 4 (over z).
Axes of the slice: x: 4, y: 4, z: 4, core: 2. Of those that a mesh axis runs over, the one named last changes fastest.
Arguments:
- out_grad: bfloat16 [512, 8192], P('dp', 'mp'), may hold values from -6 to 6
- upper_w: bfloat16 [2, 14336, 8192], P('section', 'dp', 'mp'), may hold values from -0.0625 to 0.0625
- lower_w: bfloat16 [2, 8192, 14336], P('section', 'mp', 'dp'), may hold values from -0.046875 to 0.046875
- upper_in: bfloat16 [2, 512, 14336], P('section', None, 'mp'), may hold values from -6 to 6
- lower_in: bfloat16 [2, 512, 8192], P('section', None, 'dp'), may hold values from -6 to 6
- upper_deriv: bfloat16 [2, 512, 14336], P('section', 'mp', 'dp'), may hold values from 0.3984375 to 1.5
- lower_deriv: bfloat16 [2, 512, 8192], P('section', 'dp', 'mp'), may hold values from 0.3984375 to 1.5
- proj_upper_in: bfloat16 [2, 64, 14336], P('section', None, 'mp'), may hold values from -0.046875 to 0.046875
- proj_upper_out: bfloat16 [2, 64, 8192], P('section', None, 'mp'), may hold values from -0.0625 to 0.0625
- proj_lower_in: bfloat16 [2, 64, 8192], P('section', None, 'dp'), may hold values from -0.0625 to 0.0625
- proj_lower_out: bfloat16 [2, 64, 14336], P('section', None, 'dp'), may hold values from -0.046875 to 0.046875
- window_ids: int32 [512], replicated, may hold values from 0 to 255
- window_slot: int32 [256], replicated, may hold values from 0 to 255, each once
Outputs:
- section_grads: bfloat16 [2, 512, 8192], P('section', 'dp', 'mp')
- sketches: float32 [2, 2, 256, 4096], P('section', None, ('dp', 'mp'))
The draws below stay inside these ranges and needn't reach their ends.
Inputs may be any that keep to these rules, and one draw needn't show every extreme that they name: Each window has exactly one row: window_slot is a permutation.
All inputs are finite; a program needn't handle non-finite values.
Results may differ from the reference program's by a relative error of at most 0.0075.
Values may be sent and summed in bfloat16 or wider, within the bound.
No kernel may reach another device: no remote copies, remote signals or barrier semaphores. Data moves between devices by JAX's collectives and lax.ppermute only.
A program may use at most 128 MiB of HBM per device.

```python
import math
import jax
import jax.numpy as jnp
import numpy as np
from jax import lax

D = 8192
FF = 14336
RANK = 64
TOKENS = 512
NWIN = 256
N_SECTION = 2


def place_ends(result, own_key, least, largest):
    dims = result.shape
    spot = [jax.random.randint(jax.random.fold_in(own_key, axis), (), 0, dims[axis]) for axis in range(len(dims))]
    result = result.at[tuple(spot)].set(least)
    longest = dims.index(max(dims))
    spot[longest] = (spot[longest] + 1) % dims[longest]
    return result.at[tuple(spot)].set(largest)


def block_levels(stream_key, shape, shards, least, top_value):
    def one(axis_at, parts):
        heights = jax.random.uniform(jax.random.fold_in(jax.random.fold_in(stream_key, 6), axis_at), (parts,), jnp.float32, least / len(shards), top_value / len(shards))
        return jnp.repeat(jnp.exp(heights), shape[axis_at] // parts).reshape((-1,) + (1,) * (len(shape) - axis_at - 1))

    loudness = one(*shards[0])
    for cut in shards[1:]:
        loudness = loudness * one(*cut)
    return loudness


def rank_bounds(amount, skew):
    weights = [(1 << 20) // math.isqrt(grade ** skew) + 1 for grade in range(1, amount + 1)]
    width = 1 + sum(weights) // (1 << 30)
    return np.cumsum(np.array([max(1, weight // width) for weight in weights]))


def ranked(rng, dims, amount, slope):
    listing = rank_bounds(amount, slope)
    ticket = jax.random.randint(jax.random.fold_in(rng, 1), dims, 0, int(listing[amount - 1]))
    standing = jnp.searchsorted(jnp.asarray(listing, jnp.int32), ticket, side="right")
    return jax.random.permutation(jax.random.fold_in(rng, 2), amount)[standing].astype(jnp.int32)


def noise(own_key, extent, width, limit, cuts=(), kind=jnp.bfloat16):
    entries = jax.random.normal(own_key, extent, jnp.float32) * width
    if len(cuts) > 0:
        entries = block_levels(own_key, extent, cuts, -0.22, 0.18) * entries
    return jnp.clip(entries, min=-limit, max=limit).astype(kind)


def setup_inputs(seed: int = 0) -> dict:
    key_list = jax.random.split(jax.random.key(seed), 14)
    out_grad = noise(key_list[0], (TOKENS, D), 1.0, 6.0, ((0, 16), (1, 4)))
    upper_w = noise(key_list[1], (N_SECTION, FF, D), D ** -0.5, 0.0625, ((0, 2), (1, 16), (2, 4)))
    lower_w = noise(key_list[2], (N_SECTION, D, FF), FF ** -0.5, 0.046875, ((0, 2), (1, 4), (2, 16)))
    upper_in = noise(key_list[3], (N_SECTION, TOKENS, FF), 1.0, 6.0, ((0, 2), (2, 4)))
    lower_in = noise(key_list[4], (N_SECTION, TOKENS, D), 1.0, 6.0, ((0, 2), (2, 16)))
    upper_deriv = jnp.clip(0.3984375 + 1.1015625 * jax.random.uniform(key_list[5], (N_SECTION, TOKENS, FF), jnp.float32) ** block_levels(key_list[5], (N_SECTION, TOKENS, FF), ((0, 2), (1, 4), (2, 16)), -0.2, 0.2), 0.3984375, 1.5).astype(jnp.bfloat16)
    lower_deriv = jnp.clip(0.3984375 + 1.1015625 * jax.random.uniform(key_list[6], (N_SECTION, TOKENS, D), jnp.float32) ** block_levels(key_list[6], (N_SECTION, TOKENS, D), ((0, 2), (1, 16), (2, 4)), -0.2, 0.2), 0.3984375, 1.5).astype(jnp.bfloat16)
    proj_upper_in = noise(key_list[7], (N_SECTION, RANK, FF), FF ** -0.5, 0.046875, ((0, 2), (2, 4)))
    proj_upper_out = noise(key_list[8], (N_SECTION, RANK, D), D ** -0.5, 0.0625, ((0, 2), (2, 4)))
    proj_lower_in = noise(key_list[9], (N_SECTION, RANK, D), D ** -0.5, 0.0625, ((0, 2), (2, 16)))
    proj_lower_out = noise(key_list[10], (N_SECTION, RANK, FF), FF ** -0.5, 0.046875, ((0, 2), (2, 16)))
    window_ids = place_ends(ranked(key_list[11], (TOKENS,), NWIN, 2), jax.random.fold_in(key_list[11], 3), 0, NWIN - 1).astype(jnp.int32)
    window_slot = jax.random.permutation(key_list[12], NWIN).astype(jnp.int32)
    return {"out_grad": out_grad, "upper_w": upper_w, "lower_w": lower_w, "upper_in": upper_in, "lower_in": lower_in, "upper_deriv": upper_deriv, "lower_deriv": lower_deriv, "proj_upper_in": proj_upper_in, "proj_upper_out": proj_upper_out, "proj_lower_in": proj_lower_in, "proj_lower_out": proj_lower_out, "window_ids": window_ids, "window_slot": window_slot}


def sketch_of(factors, window_ids, window_slot):
    rank_size = factors.shape[1] // 2
    target = window_slot[window_ids]
    hits = (target[:, None] == jnp.arange(window_slot.shape[0], dtype=jnp.int32)[None, :]).astype(jnp.float32)
    left = factors[:, :rank_size]
    right = factors[:, rank_size:]
    outer = (left[:, :, None] * right[:, None, :]).reshape(factors.shape[0], rank_size * rank_size)
    return jnp.dot(hits.T, outer, precision=lax.Precision.HIGHEST, preferred_element_type=jnp.float32)


def reference(out_grad, upper_w, lower_w, upper_in, lower_in, upper_deriv, lower_deriv, proj_upper_in, proj_upper_out, proj_lower_in, proj_lower_out, window_ids, window_slot):
    incoming = out_grad
    grads_list = []
    sketch_list = []
    for section_id in range(N_SECTION - 1, -1, -1):
        partial_up = jnp.dot(incoming, upper_w[section_id].T, preferred_element_type=jnp.float32)
        upper_grad = (partial_up * upper_deriv[section_id].astype(jnp.float32)).astype(jnp.bfloat16)
        partial_low = jnp.dot(upper_grad, lower_w[section_id].T, preferred_element_type=jnp.float32)
        section_grad = (partial_low * lower_deriv[section_id].astype(jnp.float32)).astype(jnp.bfloat16)
        upper_factors = jnp.concatenate([
            jnp.dot(upper_in[section_id], proj_upper_in[section_id].T, preferred_element_type=jnp.float32),
            jnp.dot(incoming, proj_upper_out[section_id].T, preferred_element_type=jnp.float32)], axis=1)
        lower_factors = jnp.concatenate([
            jnp.dot(lower_in[section_id], proj_lower_in[section_id].T, preferred_element_type=jnp.float32),
            jnp.dot(upper_grad, proj_lower_out[section_id].T, preferred_element_type=jnp.float32)], axis=1)
        sketch_list.append(jnp.stack([sketch_of(lower_factors, window_ids, window_slot),
                                      sketch_of(upper_factors, window_ids, window_slot)]))
        grads_list.append(section_grad)
        incoming = section_grad
    section_grads = jnp.stack(grads_list[::-1])
    sketches = jnp.stack(sketch_list[::-1])
    return section_grads, sketches
```

```python
import jax
import jax.numpy as jnp
from jax import lax
from jax.sharding import PartitionSpec as P

BF16 = jnp.bfloat16
F32 = jnp.float32


def times_t(left, right):
    return lax.dot_general(
        left, right, (((1,), (1,)), ((), ())), preferred_element_type=F32
    )


def swap_sections(block):
    return lax.ppermute(block, "section", [(0, 1), (1, 0)])


def shift_mp(block, distance):
    count = lax.axis_size("mp")
    return lax.ppermute(
        block, "mp", [(i, (i + distance) % count) for i in range(count)]
    )


def gather_dp(block):
    count = lax.axis_size("dp")
    copies = jnp.broadcast_to(block[None], (count,) + block.shape)
    got = lax.all_to_all(copies, "dp", 0, 0, tiled=True)
    return got.reshape(count * block.shape[0], block.shape[1])


def scatter_sum_dp(partial):
    count = lax.axis_size("dp")
    got = lax.all_to_all(partial, "dp", 0, 0, tiled=True)
    got = got.reshape(count, partial.shape[0] // count, partial.shape[1])
    return jnp.sum(got.astype(F32), axis=0)


def scatter_sum_mp(partial):
    count = lax.axis_size("mp")
    mine = lax.axis_index("mp")
    rows = partial.shape[0] // count

    def part(distance):
        return lax.dynamic_slice_in_dim(
            partial, ((mine + distance) % count) * rows, rows, 0
        )

    total = part(0).astype(F32)
    for distance in range(1, count):
        total = total + shift_mp(part(distance), distance).astype(F32)
    return total


def gather_mp(block):
    count = lax.axis_size("mp")
    mine = lax.axis_index("mp")
    rows = block.shape[0]
    whole = jnp.zeros((count * rows, block.shape[1]), block.dtype)
    whole = lax.dynamic_update_slice_in_dim(whole, block, mine * rows, 0)
    for distance in range(1, count):
        got = shift_mp(block, distance)
        whole = lax.dynamic_update_slice_in_dim(
            whole, got, ((mine - distance) % count) * rows, 0
        )
    return whole


def body(
    out_grad,
    upper_w,
    lower_w,
    upper_in,
    lower_in,
    upper_deriv,
    lower_deriv,
    proj_upper_in,
    proj_upper_out,
    proj_lower_in,
    proj_lower_out,
    window_ids,
    window_slot,
):
    sections = lax.axis_size("section")
    dp_count = lax.axis_size("dp")
    mp_count = lax.axis_size("mp")
    core = lax.axis_index("section")
    rank = proj_upper_in.shape[1]
    tokens_dp, width = out_grad.shape
    hidden = upper_deriv.shape[2]
    tokens = tokens_dp * dp_count
    half = tokens_dp // sections

    def halves(array):
        cut = array.reshape(
            array.shape[0] // tokens_dp, sections, half, array.shape[1]
        )
        mine = lax.dynamic_index_in_dim(cut, core, 1, keepdims=False)
        other = lax.dynamic_index_in_dim(cut, 1 - core, 1, keepdims=False)
        shape = (array.shape[0] // sections, array.shape[1])
        return mine.reshape(shape), other.reshape(shape)

    def exchanged(array):
        mine, other = halves(array)
        return mine, swap_sections(other)

    def of_section(pair, section):
        own, received = pair
        return jnp.where(core == section, own, received)

    grad, _ = halves(out_grad)
    first = gather_dp(grad)

    weight_up = (upper_w[0], swap_sections(upper_w[0]))
    pout_up = (proj_upper_out[0], swap_sections(proj_upper_out[0]))
    factor_up = exchanged(times_t(upper_in[0], proj_upper_in[0]).astype(BF16))
    deriv_up = exchanged(upper_deriv[0])
    weight_low = (lower_w[0], swap_sections(lower_w[0]))
    pout_low = (proj_lower_out[0], swap_sections(proj_lower_out[0]))
    factor_low = exchanged(times_t(lower_in[0], proj_lower_in[0]).astype(BF16))
    deriv_low = exchanged(lower_deriv[0])

    gathered = first
    grads = [None] * sections
    ups = [None] * sections
    lows = [None] * sections
    for section in range(sections - 1, -1, -1):
        with jax.named_scope(f"up_{section}"):
            partial = jnp.concatenate(
                [
                    times_t(gathered, of_section(weight_up, section)).astype(BF16),
                    of_section(factor_up, section),
                    times_t(gathered, of_section(pout_up, section)).astype(BF16),
                ],
                axis=1,
            )
            summed = scatter_sum_mp(partial)
            scale = of_section(deriv_up, section).astype(F32)
            middle = (summed[:, :hidden] * scale).astype(BF16)
            block = jnp.concatenate([middle, summed[:, hidden:].astype(BF16)], axis=1)
            whole = gather_mp(block)
            middle_all = whole[:, :hidden]
            ups[section] = whole[:, hidden:]
        with jax.named_scope(f"low_{section}"):
            partial = jnp.concatenate(
                [
                    times_t(middle_all, of_section(weight_low, section)).astype(BF16),
                    of_section(factor_low, section),
                    times_t(middle_all, of_section(pout_low, section)).astype(BF16),
                ],
                axis=1,
            )
            summed = scatter_sum_dp(partial)
            scale = of_section(deriv_low, section).astype(F32)
            grad = (summed[:, :width] * scale).astype(BF16)
            grads[section] = grad
            low = summed[:, width:].astype(BF16)
            if section > 0:
                got = gather_dp(jnp.concatenate([grad, low], axis=1))
                gathered = got[:, :width]
                lows[section] = got[:, width:]
            else:
                lows[section] = gather_dp(low)

    with jax.named_scope("outputs"):
        pair = [jnp.concatenate([lows[s], ups[s]], axis=1) for s in range(sections)]
        mine = jnp.where(core == 0, pair[0], pair[1])
        other = jnp.where(core == 0, pair[1], pair[0])
        got = swap_sections(other)

        def joined(own, received, rows):
            own = own.reshape(-1, rows, own.shape[1])
            received = received.reshape(-1, rows, received.shape[1])
            stack = jnp.stack(
                [
                    jnp.where(core == 0, own, received),
                    jnp.where(core == 0, received, own),
                ],
                axis=1,
            )
            return stack.reshape(-1, own.shape[2])

        factors = joined(mine, got, half)
        mine = jnp.where(core == 0, grads[0], grads[1])
        other = jnp.where(core == 0, grads[1], grads[0])
        grads_out = joined(mine, swap_sections(other), half)

        windows = window_slot.shape[0]
        owned = windows // (dp_count * mp_count)
        position = lax.axis_index("dp") * mp_count + lax.axis_index("mp")
        rows = position * owned + jnp.arange(owned, dtype=jnp.int32)
        holds = window_slot[None, :] == rows[:, None]
        window = jnp.sum(
            jnp.where(holds, jnp.arange(windows, dtype=jnp.int32)[None, :], 0), axis=1
        )
        hits = window_ids[None, :] == window[:, None]
        sketches = []
        for place in range(2):
            pair = factors[:, 2 * rank * place : 2 * rank * (place + 1)]
            left = pair[:, :rank]
            right = pair[:, rank:]
            masked = jnp.where(hits[:, :, None], left[None], jnp.zeros((), BF16))
            sums = lax.dot_general(
                masked, right, (((1,), (0,)), ((), ())), preferred_element_type=F32
            )
            sketches.append(sums.reshape(owned, rank * rank))
        sketch = jnp.stack(sketches)
    return (grads_out[None], sketch[None])


def solution(mesh):
    placed = (
        P("dp", "mp"),
        P("section", "dp", "mp"),
        P("section", "mp", "dp"),
        P("section", None, "mp"),
        P("section", None, "dp"),
        P("section", "mp", "dp"),
        P("section", "dp", "mp"),
        P("section", None, "mp"),
        P("section", None, "mp"),
        P("section", None, "dp"),
        P("section", None, "dp"),
        P(),
        P(),
    )
    return jax.shard_map(
        body,
        mesh=mesh,
        in_specs=placed,
        out_specs=(P("section", "dp", "mp"), P("section", None, ("dp", "mp"), None)),
        check_vma=False,
    )
```

```python
import jax
import jax.numpy as jnp
from jax import lax
from jax.experimental import pallas as pl
from jax.experimental.pallas import tpu as pltpu
from jax.sharding import PartitionSpec as P

BF16 = jnp.bfloat16
F32 = jnp.float32


def times_t(left, right):
    return lax.dot_general(
        left, right, (((1,), (1,)), ((), ())), preferred_element_type=F32
    )


def swap_sections(block):
    return lax.ppermute(block, "section", [(0, 1), (1, 0)])


def shift_mp(block, distance):
    count = lax.axis_size("mp")
    return lax.ppermute(
        block, "mp", [(i, (i + distance) % count) for i in range(count)]
    )


def gather_dp(block):
    count = lax.axis_size("dp")
    copies = jnp.broadcast_to(block[None], (count,) + block.shape)
    got = lax.all_to_all(copies, "dp", 0, 0, tiled=True)
    return got.reshape(count * block.shape[0], block.shape[1])


def scatter_sum_dp(partial):
    count = lax.axis_size("dp")
    got = lax.all_to_all(partial, "dp", 0, 0, tiled=True)
    got = got.reshape(count, partial.shape[0] // count, partial.shape[1])
    return jnp.sum(got.astype(F32), axis=0)


def gather_mp(block):
    count = lax.axis_size("mp")
    mine = lax.axis_index("mp")
    rows = block.shape[0]
    whole = jnp.zeros((count * rows, block.shape[1]), block.dtype)
    whole = lax.dynamic_update_slice_in_dim(whole, block, mine * rows, 0)
    for distance in range(1, count):
        got = shift_mp(block, distance)
        whole = lax.dynamic_update_slice_in_dim(
            whole, got, ((mine - distance) % count) * rows, 0
        )
    return whole


def upper_product(place, rows, own, received, tail, side, count):
    tokens, depth = rows.shape
    width = own.shape[0]
    extra = tail.shape[0]
    size = tokens // count
    step = depth // 4

    def kernel(place_ref, x_ref, own_ref, got_ref, tail_ref, side_ref, *rest):
        outs, acc = rest[:count], rest[count]
        k = pl.program_id(0)

        @pl.when(k == 0)
        def _():
            acc[:, :width] = jnp.zeros((tokens, width), F32)
            acc[:, width:] = side_ref[...].astype(F32)

        @pl.when(place_ref[0] == 1)
        def _():
            acc[:, :width] += times_t(x_ref[...], own_ref[...])

        @pl.when(place_ref[0] != 1)
        def _():
            acc[:, :width] += times_t(x_ref[...], got_ref[...])

        acc[:, width:] += times_t(x_ref[...], tail_ref[...])

        @pl.when(k == pl.num_programs(0) - 1)
        def _():
            for d in range(count):
                first = pl.multiple_of(lax.rem(place_ref[1] + d, count) * size, size)
                outs[d][...] = acc[pl.ds(first, size), :].astype(BF16)

    return pl.pallas_call(
        kernel,
        out_shape=[jax.ShapeDtypeStruct((size, width + extra), BF16)] * count,
        grid_spec=pltpu.PrefetchScalarGridSpec(
            num_scalar_prefetch=1,
            grid=(4,),
            in_specs=[
                pl.BlockSpec((tokens, step), lambda k, p: (0, k)),
                pl.BlockSpec((width, step), lambda k, p: (0, k * p[0])),
                pl.BlockSpec((width, step), lambda k, p: (0, k * (1 - p[0]))),
                pl.BlockSpec((extra, step), lambda k, p: (0, k)),
                pl.BlockSpec((tokens, extra), lambda k, p: (0, 0)),
            ],
            out_specs=[pl.BlockSpec((size, width + extra), lambda k, p: (0, 0))]
            * count,
            scratch_shapes=[pltpu.VMEM((tokens, width + extra), F32)],
        ),
        name="upper_product",
    )(place, rows, own, received, tail, side)


def lower_product(place, blocks, own, received, tail=None, side=None):
    count = len(blocks)
    size = blocks[0].shape[0]
    width, depth = own.shape
    rest_width = blocks[0].shape[1] - depth
    tokens = count * size
    extra = 0 if tail is None else tail.shape[0]
    step = width // 4

    def kernel(place_ref, *refs):
        block_refs = refs[:count]
        own_ref, got_ref = refs[count : count + 2]
        more = refs[count + 2 :]
        if extra:
            tail_ref, side_ref = more[:2]
            more = more[2:]
        out, rest_out, x_ref = more
        n = pl.program_id(0)

        @pl.when(n == 0)
        def _():
            for d in range(count):
                first = lax.rem(place_ref[1] + count - d, count) * size
                first = pl.multiple_of(first, size)
                x_ref[pl.ds(first, size), :] = block_refs[d][:, :depth]
                rest_out[pl.ds(first, size), :] = block_refs[d][:, depth:]
            if extra:
                out[:, width:] = (
                    side_ref[...].astype(F32) + times_t(x_ref[...], tail_ref[...])
                ).astype(BF16)

        here = pl.ds(pl.multiple_of(n * step, step), step)

        @pl.when(place_ref[0] == 1)
        def _():
            out[:, here] = times_t(x_ref[...], own_ref[...]).astype(BF16)

        @pl.when(place_ref[0] != 1)
        def _():
            out[:, here] = times_t(x_ref[...], got_ref[...]).astype(BF16)

    whole = lambda n, p: (0, 0)
    in_specs = [pl.BlockSpec(blocks[0].shape, whole)] * count + [
        pl.BlockSpec((step, depth), lambda n, p: (n * p[0], 0)),
        pl.BlockSpec((step, depth), lambda n, p: (n * (1 - p[0]), 0)),
    ]
    operands = list(blocks) + [own, received]
    if extra:
        in_specs += [pl.BlockSpec(tail.shape, whole), pl.BlockSpec(side.shape, whole)]
        operands += [tail, side]
    return pl.pallas_call(
        kernel,
        out_shape=[
            jax.ShapeDtypeStruct((tokens, width + extra), BF16),
            jax.ShapeDtypeStruct((tokens, rest_width), BF16),
        ],
        grid_spec=pltpu.PrefetchScalarGridSpec(
            num_scalar_prefetch=1,
            grid=(4,),
            in_specs=in_specs,
            out_specs=[
                pl.BlockSpec((tokens, width + extra), whole),
                pl.BlockSpec((tokens, rest_width), whole),
            ],
            scratch_shapes=[pltpu.VMEM((tokens, depth), BF16)],
        ),
        name="lower_product",
    )(place, *operands)


def body(
    out_grad,
    upper_w,
    lower_w,
    upper_in,
    lower_in,
    upper_deriv,
    lower_deriv,
    proj_upper_in,
    proj_upper_out,
    proj_lower_in,
    proj_lower_out,
    window_ids,
    window_slot,
):
    sections = lax.axis_size("section")
    dp_count = lax.axis_size("dp")
    mp_count = lax.axis_size("mp")
    core = lax.axis_index("section")
    rank = proj_upper_in.shape[1]
    tokens_dp, width = out_grad.shape
    hidden = upper_deriv.shape[2]
    tokens = tokens_dp * dp_count
    half = tokens_dp // sections

    def halves(array):
        cut = array.reshape(
            array.shape[0] // tokens_dp, sections, half, array.shape[1]
        )
        mine = lax.dynamic_index_in_dim(cut, core, 1, keepdims=False)
        other = lax.dynamic_index_in_dim(cut, 1 - core, 1, keepdims=False)
        shape = (array.shape[0] // sections, array.shape[1])
        return mine.reshape(shape), other.reshape(shape)

    def exchanged(array):
        mine, other = halves(array)
        return mine, swap_sections(other)

    def of_section(pair, section):
        own, received = pair
        return jnp.where(core == section, own, received)

    grad, _ = halves(out_grad)
    gathered = gather_dp(grad)
    mp_index = lax.axis_index("mp")

    def padded(array, before, after, axis):
        pads = [(0, 0), (0, 0)]
        pads[axis] = (before, after)
        return jnp.pad(array, pads)

    weight_up = (upper_w[0], swap_sections(upper_w[0]))
    pout_up = (proj_upper_out[0], swap_sections(proj_upper_out[0]))
    factor_up = exchanged(times_t(upper_in[0], proj_upper_in[0]).astype(BF16))
    factor_low = exchanged(times_t(lower_in[0], proj_lower_in[0]).astype(BF16))
    deriv_up = exchanged(upper_deriv[0])
    low_w, pout_w, deriv_w, gathered = lax.optimization_barrier(
        (lower_w[0], proj_lower_out[0], lower_deriv[0], gathered)
    )
    weight_low = (low_w, swap_sections(low_w))
    pout_low = (pout_w, swap_sections(pout_w))
    deriv_low = exchanged(deriv_w)

    grads = [None] * sections
    ups = [None] * sections
    lows = [None] * sections
    for section in range(sections - 1, -1, -1):
        place = jnp.stack([(core == section).astype(jnp.int32), mp_index])
        with jax.named_scope(f"up_{section}"):
            parts = upper_product(
                place,
                gathered[:, :width],
                *weight_up,
                padded(of_section(pout_up, section), rank, 0, 0),
                padded(of_section(factor_up, section), 0, rank, 1),
                mp_count,
            )
            summed = parts[0].astype(F32)
            for distance in range(1, mp_count):
                summed += shift_mp(parts[distance], distance).astype(F32)
            scale = of_section(deriv_up, section).astype(F32)
            middle = (summed[:, :hidden] * scale).astype(BF16)
            block = jnp.concatenate([middle, summed[:, hidden:].astype(BF16)], axis=1)
            blocks = [block] + [shift_mp(block, d) for d in range(1, mp_count)]
        with jax.named_scope(f"low_{section}"):
            scale = of_section(deriv_low, section).astype(F32)
            pout = of_section(pout_low, section)
            if section > 0:
                side = [of_section(factor_low, s) for s in range(section, -1, -1)]
                side = jnp.concatenate(
                    [padded(part, 0, rank, 1) for part in side], axis=1
                )
                tail = padded(pout, rank, side.shape[1] - 2 * rank, 0)
                partial, ups[section] = lower_product(
                    place, blocks, *weight_low, tail, side
                )
                summed = scatter_sum_dp(partial)
                grad = (summed[:, :width] * scale).astype(BF16)
                low = summed[:, width:].astype(BF16)
                gathered = gather_dp(jnp.concatenate([grad, low], axis=1))
                lows[section] = gathered[:, width : width + 2 * rank]
                left_low = gathered[:, width + 2 * rank : width + 3 * rank]
            else:
                right = gather_dp(times_t(middle, pout).astype(BF16))
                right = right.reshape(dp_count, middle.shape[0], rank)
                right = jnp.sum(right.astype(F32), axis=0).astype(BF16)
                partial, ups[section] = lower_product(place, blocks, *weight_low)
                summed = scatter_sum_dp(partial)
                grad = (summed * scale).astype(BF16)
                lows[section] = jnp.concatenate([left_low, gather_mp(right)], axis=1)
            grads[section] = grad

    with jax.named_scope("outputs"):
        pair = [jnp.concatenate([lows[s], ups[s]], axis=1) for s in range(sections)]
        mine = jnp.where(core == 0, pair[0], pair[1])
        other = jnp.where(core == 0, pair[1], pair[0])
        got = swap_sections(other)

        def joined(own, received, rows):
            own = own.reshape(-1, rows, own.shape[1])
            received = received.reshape(-1, rows, received.shape[1])
            stack = jnp.stack(
                [
                    jnp.where(core == 0, own, received),
                    jnp.where(core == 0, received, own),
                ],
                axis=1,
            )
            return stack.reshape(-1, own.shape[2])

        factors = joined(mine, got, half)
        mine = jnp.where(core == 0, grads[0], grads[1])
        other = jnp.where(core == 0, grads[1], grads[0])
        grads_out = joined(mine, swap_sections(other), half)

        windows = window_slot.shape[0]
        owned = windows // (dp_count * mp_count)
        position = lax.axis_index("dp") * mp_count + lax.axis_index("mp")
        rows = position * owned + jnp.arange(owned, dtype=jnp.int32)
        holds = window_slot[None, :] == rows[:, None]
        window = jnp.sum(
            jnp.where(holds, jnp.arange(windows, dtype=jnp.int32)[None, :], 0), axis=1
        )
        hits = window_ids[None, :] == window[:, None]
        sketches = []
        for place in range(2):
            pair = factors[:, 2 * rank * place : 2 * rank * (place + 1)]
            left = pair[:, :rank]
            right = pair[:, rank:]
            masked = jnp.where(hits[:, :, None], left[None], jnp.zeros((), BF16))
            sums = lax.dot_general(
                masked, right, (((1,), (0,)), ((), ())), preferred_element_type=F32
            )
            sketches.append(sums.reshape(owned, rank * rank))
        sketch = jnp.stack(sketches)
    return (grads_out[None], sketch[None])


def solution(mesh):
    placed = (
        P("dp", "mp"),
        P("section", "dp", "mp"),
        P("section", "mp", "dp"),
        P("section", None, "mp"),
        P("section", None, "dp"),
        P("section", "mp", "dp"),
        P("section", "dp", "mp"),
        P("section", None, "mp"),
        P("section", None, "mp"),
        P("section", None, "dp"),
        P("section", None, "dp"),
        P(),
        P(),
    )
    return jax.shard_map(
        body,
        mesh=mesh,
        in_specs=placed,
        out_specs=(P("section", "dp", "mp"), P("section", None, ("dp", "mp"), None)),
        check_vma=False,
    )
```

```python
import jax
import jax.numpy as jnp
from jax import lax
from jax.sharding import PartitionSpec as P

BF16 = jnp.bfloat16
F32 = jnp.float32


def times_t(left, right):
    return lax.dot_general(
        left, right, (((1,), (1,)), ((), ())), preferred_element_type=F32
    )


def swap_sections(block):
    return lax.ppermute(block, "section", [(0, 1), (1, 0)])


def shift_mp(block, distance):
    count = lax.axis_size("mp")
    return lax.ppermute(
        block, "mp", [(i, (i + distance) % count) for i in range(count)]
    )


def gather_dp(block):
    count = lax.axis_size("dp")
    copies = jnp.broadcast_to(block[None], (count,) + block.shape)
    got = lax.all_to_all(copies, "dp", 0, 0, tiled=True)
    return got.reshape(count * block.shape[0], block.shape[1])


def scatter_sum_dp(partial):
    count = lax.axis_size("dp")
    got = lax.all_to_all(partial, "dp", 0, 0, tiled=True)
    got = got.reshape(count, partial.shape[0] // count, partial.shape[1])
    return jnp.sum(got.astype(F32), axis=0)


def from_all_mp(block):
    count = lax.axis_size("mp")
    return [block] + [shift_mp(block, distance) for distance in range(1, count)]


def scatter_sum_mp(partial):
    count = lax.axis_size("mp")
    mine = lax.axis_index("mp")
    rows = partial.shape[0] // count

    def part(distance):
        return lax.dynamic_slice_in_dim(
            partial, ((mine + distance) % count) * rows, rows, 0
        )

    total = part(0).astype(F32)
    for distance in range(1, count):
        total = total + shift_mp(part(distance), distance).astype(F32)
    return total


def gather_mp(block):
    count = lax.axis_size("mp")
    mine = lax.axis_index("mp")
    rows = block.shape[0]
    whole = jnp.zeros((count * rows, block.shape[1]), block.dtype)
    for distance, got in enumerate(from_all_mp(block)):
        whole = lax.dynamic_update_slice_in_dim(
            whole, got, ((mine - distance) % count) * rows, 0
        )
    return whole


def body(
    out_grad,
    upper_w,
    lower_w,
    upper_in,
    lower_in,
    upper_deriv,
    lower_deriv,
    proj_upper_in,
    proj_upper_out,
    proj_lower_in,
    proj_lower_out,
    window_ids,
    window_slot,
):
    sections = lax.axis_size("section")
    dp_count = lax.axis_size("dp")
    mp_count = lax.axis_size("mp")
    core = lax.axis_index("section")
    rank = proj_upper_in.shape[1]
    tokens_dp, width = out_grad.shape
    hidden = upper_deriv.shape[2]
    tokens = tokens_dp * dp_count
    half = tokens_dp // sections

    def halves(array):
        cut = array.reshape(
            array.shape[0] // tokens_dp, sections, half, array.shape[1]
        )
        mine = lax.dynamic_index_in_dim(cut, core, 1, keepdims=False)
        other = lax.dynamic_index_in_dim(cut, 1 - core, 1, keepdims=False)
        shape = (array.shape[0] // sections, array.shape[1])
        return mine.reshape(shape), other.reshape(shape)

    def swapped(*arrays):
        got = swap_sections(jnp.concatenate(arrays, axis=0))
        cuts = []
        for array in arrays[:-1]:
            cuts.append((cuts[-1] if cuts else 0) + array.shape[0])
        return jnp.split(got, cuts, axis=0)

    def of_section(pair, section):
        own, received = pair
        return jnp.where(core == section, own, received)

    def held(*arrays):
        return lax.optimization_barrier(arrays)

    dp_index = lax.axis_index("dp")
    mp_index = lax.axis_index("mp")
    tokens_mp = upper_deriv.shape[1]

    grad, _ = halves(out_grad)
    gathered = gather_dp(grad)

    deriv_up, deriv_up_sent = halves(upper_deriv[0])
    deriv_low, deriv_low_sent = halves(lower_deriv[0])
    left_up, left_up_sent = halves(
        times_t(
            lax.dynamic_slice_in_dim(upper_in[0], dp_index * tokens_dp, tokens_dp, 0),
            proj_upper_in[0],
        ).astype(BF16)
    )
    left_low, left_low_sent = halves(
        times_t(
            lax.dynamic_slice_in_dim(lower_in[0], mp_index * tokens_mp, tokens_mp, 0),
            proj_lower_in[0],
        ).astype(BF16)
    )
    weight_up = (upper_w[0], swap_sections(upper_w[0]))
    got = swapped(proj_upper_out[0], deriv_low_sent)
    pout_up = (proj_upper_out[0], got[0])
    deriv_low = (deriv_low, got[1])
    got = swapped(left_up_sent, left_low_sent)
    left_up = (left_up, got[0])
    left_low = (left_low, got[1])
    got = swapped(proj_lower_out[0], deriv_up_sent)
    pout_low = (proj_lower_out[0], got[0])
    deriv_up = (deriv_up, got[1])
    weight_low = (lower_w[0], swap_sections(lower_w[0]))

    last = sections - 1
    grads = [None] * sections
    ups = []
    lows = []
    for section in range(last, -1, -1):
        with jax.named_scope(f"up_{section}"):
            up = [times_t(grad, of_section(pout_up, section)).astype(BF16)]
            if section == last:
                up += [of_section(left_up, s) for s in range(last, -1, -1)]
            up = from_all_mp(jnp.concatenate(up, axis=1))
            up = sum(part.astype(F32) for part in up).astype(BF16)
            weight = of_section(weight_up, section)
            summed = scatter_sum_mp(times_t(gathered, weight).astype(BF16))
            scale = of_section(deriv_up, section).astype(F32)
            middle = (summed * scale).astype(BF16)
        with jax.named_scope(f"low_{section}"):
            low = [times_t(middle, of_section(pout_low, section)).astype(BF16)]
            if section == last:
                low += [of_section(left_low, s) for s in range(last, -1, -1)]
            ups.append(up)
            lows += low
            if section == 0:
                low = jnp.concatenate(lows, axis=1)
                up = jnp.concatenate(ups, axis=1)
                rows = low.shape[0]
                both = gather_dp(jnp.concatenate([low, up], axis=0))
                both = both.reshape(dp_count, rows + up.shape[0], up.shape[1])
                low = jnp.sum(both[:, :rows].astype(F32), axis=0).astype(BF16)
                up = both[:, rows:].reshape(tokens // sections, up.shape[1])

            middle_all = gather_mp(middle)
            weight = of_section(weight_low, section)
            partial = times_t(middle_all, weight).astype(BF16)
            if section == 0:
                low, up, partial = held(low, up, partial)
            summed = scatter_sum_dp(partial)
            scale = of_section(deriv_low, section).astype(F32)
            grad = (summed * scale).astype(BF16)
            grads[section] = grad
            if section > 0:
                gathered = gather_dp(grad)

    with jax.named_scope("outputs"):
        low = gather_mp(low)

        def columns(array, section):
            turn = last - section
            left = 1 + turn
            right = 0 if turn == 0 else sections + turn
            return [
                array[:, left * rank : (left + 1) * rank],
                array[:, right * rank : (right + 1) * rank],
            ]

        pair = [
            jnp.concatenate(columns(low, s) + columns(up, s), axis=1)
            for s in range(sections)
        ]
        mine = jnp.where(core == 0, pair[0], pair[1])
        other = jnp.where(core == 0, pair[1], pair[0])
        other, grads[0] = held(other, grads[0])
        got = swap_sections(other)

        def joined(own, received, rows):
            own = own.reshape(-1, rows, own.shape[1])
            received = received.reshape(-1, rows, received.shape[1])
            stack = jnp.stack(
                [
                    jnp.where(core == 0, own, received),
                    jnp.where(core == 0, received, own),
                ],
                axis=1,
            )
            return stack.reshape(-1, own.shape[2])

        factors = joined(mine, got, half)
        mine = jnp.where(core == 0, grads[0], grads[1])
        other = jnp.where(core == 0, grads[1], grads[0])
        grads_out = joined(mine, swap_sections(other), half)

        windows = window_slot.shape[0]
        owned = windows // (dp_count * mp_count)
        position = lax.axis_index("dp") * mp_count + lax.axis_index("mp")
        rows = position * owned + jnp.arange(owned, dtype=jnp.int32)
        holds = window_slot[None, :] == rows[:, None]
        window = jnp.sum(
            jnp.where(holds, jnp.arange(windows, dtype=jnp.int32)[None, :], 0), axis=1
        )
        hits = window_ids[None, :] == window[:, None]
        sketches = []
        for place in range(2):
            pair = factors[:, 2 * rank * place : 2 * rank * (place + 1)]
            left = pair[:, :rank]
            right = pair[:, rank:]
            masked = jnp.where(hits[:, :, None], left[None], jnp.zeros((), BF16))
            sums = lax.dot_general(
                masked, right, (((1,), (0,)), ((), ())), preferred_element_type=F32
            )
            sketches.append(sums.reshape(owned, rank * rank))
        sketch = jnp.stack(sketches)
    return (grads_out[None], sketch[None])


def solution(mesh):
    placed = (
        P("dp", "mp"),
        P("section", "dp", "mp"),
        P("section", "mp", "dp"),
        P("section", None, "mp"),
        P("section", None, "dp"),
        P("section", "mp", "dp"),
        P("section", "dp", "mp"),
        P("section", None, "mp"),
        P("section", None, "mp"),
        P("section", None, "dp"),
        P("section", None, "dp"),
        P(),
        P(),
    )
    return jax.shard_map(
        body,
        mesh=mesh,
        in_specs=placed,
        out_specs=(P("section", "dp", "mp"), P("section", None, ("dp", "mp"), None)),
        check_vma=False,
    )
```

```python
import jax
import jax.numpy as jnp
from jax import lax
from jax.sharding import PartitionSpec as P

BF16 = jnp.bfloat16
F32 = jnp.float32


def times_t(left, right):
    return lax.dot_general(
        left, right, (((1,), (1,)), ((), ())), preferred_element_type=F32
    )


def swap_sections(block):
    return lax.ppermute(block, "section", [(0, 1), (1, 0)])


def shift_mp(block, distance):
    count = lax.axis_size("mp")
    return lax.ppermute(
        block, "mp", [(i, (i + distance) % count) for i in range(count)]
    )


def gather_dp(block):
    count = lax.axis_size("dp")
    copies = jnp.broadcast_to(block[None], (count,) + block.shape)
    got = lax.all_to_all(copies, "dp", 0, 0, tiled=True)
    return got.reshape(count * block.shape[0], block.shape[1])


def scatter_sum_dp(partial):
    count = lax.axis_size("dp")
    got = lax.all_to_all(partial, "dp", 0, 0, tiled=True)
    got = got.reshape(count, partial.shape[0] // count, partial.shape[1])
    return jnp.sum(got.astype(F32), axis=0)


def from_all_mp(block):
    count = lax.axis_size("mp")
    return [block] + [shift_mp(block, distance) for distance in range(1, count)]


def scatter_sum_mp(partial):
    count = lax.axis_size("mp")
    mine = lax.axis_index("mp")
    rows = partial.shape[0] // count

    def part(distance):
        return lax.dynamic_slice_in_dim(
            partial, ((mine + distance) % count) * rows, rows, 0
        )

    total = part(0).astype(F32)
    for distance in range(1, count):
        total = total + shift_mp(part(distance), distance).astype(F32)
    return total


def gather_mp(block):
    count = lax.axis_size("mp")
    mine = lax.axis_index("mp")
    rows = block.shape[0]
    whole = jnp.zeros((count * rows, block.shape[1]), block.dtype)
    for distance, got in enumerate(from_all_mp(block)):
        whole = lax.dynamic_update_slice_in_dim(
            whole, got, ((mine - distance) % count) * rows, 0
        )
    return whole


def body(
    out_grad,
    upper_w,
    lower_w,
    upper_in,
    lower_in,
    upper_deriv,
    lower_deriv,
    proj_upper_in,
    proj_upper_out,
    proj_lower_in,
    proj_lower_out,
    window_ids,
    window_slot,
):
    sections = lax.axis_size("section")
    dp_count = lax.axis_size("dp")
    mp_count = lax.axis_size("mp")
    core = lax.axis_index("section")
    rank = proj_upper_in.shape[1]
    tokens_dp, width = out_grad.shape
    hidden = upper_deriv.shape[2]
    tokens = tokens_dp * dp_count
    half = tokens_dp // sections

    def halves(array):
        cut = array.reshape(
            array.shape[0] // tokens_dp, sections, half, array.shape[1]
        )
        mine = lax.dynamic_index_in_dim(cut, core, 1, keepdims=False)
        other = lax.dynamic_index_in_dim(cut, 1 - core, 1, keepdims=False)
        shape = (array.shape[0] // sections, array.shape[1])
        return mine.reshape(shape), other.reshape(shape)

    def swapped(*arrays):
        got = swap_sections(jnp.concatenate(arrays, axis=0))
        cuts = []
        for array in arrays[:-1]:
            cuts.append((cuts[-1] if cuts else 0) + array.shape[0])
        return jnp.split(got, cuts, axis=0)

    def of_section(pair, section):
        own, received = pair
        return jnp.where(core == section, own, received)

    def held(*arrays):
        return lax.optimization_barrier(arrays)

    dp_index = lax.axis_index("dp")
    mp_index = lax.axis_index("mp")
    tokens_mp = upper_deriv.shape[1]

    grad, _ = halves(out_grad)
    gathered = gather_dp(grad)

    deriv_up, deriv_up_sent = halves(upper_deriv[0])
    deriv_low, deriv_low_sent = halves(lower_deriv[0])
    left_up, left_up_sent = halves(
        times_t(
            lax.dynamic_slice_in_dim(upper_in[0], dp_index * tokens_dp, tokens_dp, 0),
            proj_upper_in[0],
        ).astype(BF16)
    )
    left_low, left_low_sent = halves(
        times_t(
            lax.dynamic_slice_in_dim(lower_in[0], mp_index * tokens_mp, tokens_mp, 0),
            proj_lower_in[0],
        ).astype(BF16)
    )
    weight_up = (upper_w[0], swap_sections(upper_w[0]))
    got = swapped(proj_upper_out[0], deriv_low_sent)
    pout_up = (proj_upper_out[0], got[0])
    deriv_low = (deriv_low, got[1])
    got = swapped(left_up_sent, left_low_sent)
    left_up = (left_up, got[0])
    left_low = (left_low, got[1])
    got = swapped(proj_lower_out[0], deriv_up_sent)
    pout_low = (proj_lower_out[0], got[0])
    deriv_up = (deriv_up, got[1])
    weight_low = (lower_w[0], swap_sections(lower_w[0]))

    last = sections - 1
    grads = [None] * sections
    ups = []
    lows = []
    for section in range(last, -1, -1):
        with jax.named_scope(f"up_{section}"):
            ups.append(times_t(grad, of_section(pout_up, section)).astype(BF16))
            if section == last:
                ups += [of_section(left_up, s) for s in range(last, -1, -1)]
            if section == 0:
                up = from_all_mp(jnp.concatenate(ups, axis=1))
                up = sum(part.astype(F32) for part in up).astype(BF16)
            weight = of_section(weight_up, section)
            summed = scatter_sum_mp(times_t(gathered, weight).astype(BF16))
            scale = of_section(deriv_up, section).astype(F32)
            middle = (summed * scale).astype(BF16)
        with jax.named_scope(f"low_{section}"):
            low = [times_t(middle, of_section(pout_low, section)).astype(BF16)]
            if section == last:
                low += [of_section(left_low, s) for s in range(last, -1, -1)]
            lows += low
            if section == 0:
                low = jnp.concatenate(lows, axis=1)
                rows = low.shape[0]
                both = gather_dp(jnp.concatenate([low, up], axis=0))
                both = both.reshape(dp_count, rows + up.shape[0], up.shape[1])
                low = jnp.sum(both[:, :rows].astype(F32), axis=0).astype(BF16)
                up = both[:, rows:].reshape(tokens // sections, up.shape[1])

            middle_all = gather_mp(middle)
            weight = of_section(weight_low, section)
            partial = times_t(middle_all, weight).astype(BF16)
            if section == 0:
                low, up, partial = held(low, up, partial)
            summed = scatter_sum_dp(partial)
            scale = of_section(deriv_low, section).astype(F32)
            grad = (summed * scale).astype(BF16)
            grads[section] = grad
            if section > 0:
                gathered = gather_dp(grad)

    with jax.named_scope("outputs"):
        low = gather_mp(low)

        def columns(array, section):
            turn = last - section
            left = 1 + turn
            right = 0 if turn == 0 else sections + turn
            return [
                array[:, left * rank : (left + 1) * rank],
                array[:, right * rank : (right + 1) * rank],
            ]

        pair = [
            jnp.concatenate(columns(low, s) + columns(up, s), axis=1)
            for s in range(sections)
        ]
        mine = jnp.where(core == 0, pair[0], pair[1])
        other = jnp.where(core == 0, pair[1], pair[0])
        other, grads[0] = held(other, grads[0])
        got = swap_sections(other)

        def joined(own, received, rows):
            own = own.reshape(-1, rows, own.shape[1])
            received = received.reshape(-1, rows, received.shape[1])
            stack = jnp.stack(
                [
                    jnp.where(core == 0, own, received),
                    jnp.where(core == 0, received, own),
                ],
                axis=1,
            )
            return stack.reshape(-1, own.shape[2])

        factors = joined(mine, got, half)
        mine = jnp.where(core == 0, grads[0], grads[1])
        other = jnp.where(core == 0, grads[1], grads[0])
        grads_out = joined(mine, swap_sections(other), half)

        windows = window_slot.shape[0]
        owned = windows // (dp_count * mp_count)
        position = lax.axis_index("dp") * mp_count + lax.axis_index("mp")
        rows = position * owned + jnp.arange(owned, dtype=jnp.int32)
        holds = window_slot[None, :] == rows[:, None]
        window = jnp.sum(
            jnp.where(holds, jnp.arange(windows, dtype=jnp.int32)[None, :], 0), axis=1
        )
        hits = window_ids[None, :] == window[:, None]
        sketches = []
        for place in range(2):
            pair = factors[:, 2 * rank * place : 2 * rank * (place + 1)]
            left = pair[:, :rank]
            right = pair[:, rank:]
            masked = jnp.where(hits[:, :, None], left[None], jnp.zeros((), BF16))
            sums = lax.dot_general(
                masked, right, (((1,), (0,)), ((), ())), preferred_element_type=F32
            )
            sketches.append(sums.reshape(owned, rank * rank))
        sketch = jnp.stack(sketches)
    return (grads_out[None], sketch[None])


def solution(mesh):
    placed = (
        P("dp", "mp"),
        P("section", "dp", "mp"),
        P("section", "mp", "dp"),
        P("section", None, "mp"),
        P("section", None, "dp"),
        P("section", "mp", "dp"),
        P("section", "dp", "mp"),
        P("section", None, "mp"),
        P("section", None, "mp"),
        P("section", None, "dp"),
        P("section", None, "dp"),
        P(),
        P(),
    )
    return jax.shard_map(
        body,
        mesh=mesh,
        in_specs=placed,
        out_specs=(P("section", "dp", "mp"), P("section", None, ("dp", "mp"), None)),
        check_vma=False,
    )
```

```python
import jax
import jax.numpy as jnp
from jax import lax
from jax.sharding import PartitionSpec as P

BF16 = jnp.bfloat16
F32 = jnp.float32


def times_t(left, right):
    return lax.dot_general(
        left, right, (((1,), (1,)), ((), ())), preferred_element_type=F32
    )


def swap_sections(block):
    return lax.ppermute(block, "section", [(0, 1), (1, 0)])


def shift_mp(block, distance):
    count = lax.axis_size("mp")
    return lax.ppermute(
        block, "mp", [(i, (i + distance) % count) for i in range(count)]
    )


def gather_dp(block):
    count = lax.axis_size("dp")
    copies = jnp.broadcast_to(block[None], (count,) + block.shape)
    got = lax.all_to_all(copies, "dp", 0, 0, tiled=True)
    return got.reshape(count * block.shape[0], block.shape[1])


def scatter_sum_dp(partial):
    count = lax.axis_size("dp")
    got = lax.all_to_all(partial, "dp", 0, 0, tiled=True)
    got = got.reshape(count, partial.shape[0] // count, partial.shape[1])
    return jnp.sum(got.astype(F32), axis=0)


def from_all_mp(block):
    count = lax.axis_size("mp")
    return [block] + [shift_mp(block, distance) for distance in range(1, count)]


def scatter_sum_mp(partial):
    count = lax.axis_size("mp")
    mine = lax.axis_index("mp")
    rows = partial.shape[0] // count

    def part(distance):
        return lax.dynamic_slice_in_dim(
            partial, ((mine + distance) % count) * rows, rows, 0
        )

    total = part(0).astype(F32)
    for distance in range(1, count):
        total = total + shift_mp(part(distance), distance).astype(F32)
    return total


def gather_mp(block):
    count = lax.axis_size("mp")
    mine = lax.axis_index("mp")
    rows = block.shape[0]
    whole = jnp.zeros((count * rows, block.shape[1]), block.dtype)
    for distance, got in enumerate(from_all_mp(block)):
        whole = lax.dynamic_update_slice_in_dim(
            whole, got, ((mine - distance) % count) * rows, 0
        )
    return whole


def body(
    out_grad,
    upper_w,
    lower_w,
    upper_in,
    lower_in,
    upper_deriv,
    lower_deriv,
    proj_upper_in,
    proj_upper_out,
    proj_lower_in,
    proj_lower_out,
    window_ids,
    window_slot,
):
    sections = lax.axis_size("section")
    dp_count = lax.axis_size("dp")
    mp_count = lax.axis_size("mp")
    core = lax.axis_index("section")
    rank = proj_upper_in.shape[1]
    tokens_dp, width = out_grad.shape
    hidden = upper_deriv.shape[2]
    tokens = tokens_dp * dp_count
    half = tokens_dp // sections

    def halves(array):
        cut = array.reshape(
            array.shape[0] // tokens_dp, sections, half, array.shape[1]
        )
        mine = lax.dynamic_index_in_dim(cut, core, 1, keepdims=False)
        other = lax.dynamic_index_in_dim(cut, 1 - core, 1, keepdims=False)
        shape = (array.shape[0] // sections, array.shape[1])
        return mine.reshape(shape), other.reshape(shape)

    def swapped(*arrays):
        got = swap_sections(jnp.concatenate(arrays, axis=0))
        cuts = []
        for array in arrays[:-1]:
            cuts.append((cuts[-1] if cuts else 0) + array.shape[0])
        return jnp.split(got, cuts, axis=0)

    def of_section(pair, section):
        own, received = pair
        return jnp.where(core == section, own, received)

    def held(*arrays):
        return lax.optimization_barrier(arrays)

    dp_index = lax.axis_index("dp")
    mp_index = lax.axis_index("mp")
    tokens_mp = upper_deriv.shape[1]

    grad = jnp.where(core == 0, out_grad[:half], out_grad[half:])
    gathered = gather_dp(grad)

    deriv_up, deriv_up_sent = halves(upper_deriv[0])
    deriv_low, deriv_low_sent = halves(lower_deriv[0])
    left_up, left_up_sent = halves(
        times_t(
            lax.dynamic_slice_in_dim(upper_in[0], dp_index * tokens_dp, tokens_dp, 0),
            proj_upper_in[0],
        ).astype(BF16)
    )
    left_low, left_low_sent = halves(
        times_t(
            lax.dynamic_slice_in_dim(lower_in[0], mp_index * tokens_mp, tokens_mp, 0),
            proj_lower_in[0],
        ).astype(BF16)
    )
    weight_up = (upper_w[0], swap_sections(upper_w[0]))
    got = swapped(proj_upper_out[0], deriv_low_sent)
    pout_up = (proj_upper_out[0], got[0])
    deriv_low = (deriv_low, got[1])
    got = swapped(left_up_sent, left_low_sent)
    left_up = (left_up, got[0])
    left_low = (left_low, got[1])
    got = swapped(proj_lower_out[0], deriv_up_sent)
    pout_low = (proj_lower_out[0], got[0])
    deriv_up = (deriv_up, got[1])
    weight_low = (lower_w[0], swap_sections(lower_w[0]))

    last = sections - 1
    scales_low = held(*[of_section(deriv_low, s).astype(F32) for s in range(sections)])
    grads = [None] * sections
    ups = []
    lows = []
    for section in range(last, -1, -1):
        with jax.named_scope(f"up_{section}"):
            ups.append(times_t(grad, of_section(pout_up, section)).astype(BF16))
            if section == last:
                ups += [of_section(left_up, s) for s in range(last, -1, -1)]
            if section == 0:
                up = from_all_mp(jnp.concatenate(ups, axis=1))
                up = sum(part.astype(F32) for part in up).astype(BF16)
            weight = of_section(weight_up, section)
            weight_last = of_section(weight_low, section)
            if section == last:
                weight, weight_last, gathered = held(weight, weight_last, gathered)
            summed = scatter_sum_mp(times_t(gathered, weight).astype(BF16))
            scale = of_section(deriv_up, section).astype(F32)
            middle = (summed * scale).astype(BF16)
        with jax.named_scope(f"low_{section}"):
            low = [times_t(middle, of_section(pout_low, section)).astype(BF16)]
            if section == last:
                low += [of_section(left_low, s) for s in range(last, -1, -1)]
            lows += low
            if section == 0:
                low = jnp.concatenate(lows, axis=1)
                rows = low.shape[0]
                both = gather_dp(jnp.concatenate([low, up], axis=0))
                both = both.reshape(dp_count, rows + up.shape[0], up.shape[1])
                low = jnp.sum(both[:, :rows].astype(F32), axis=0).astype(BF16)
                up = both[:, rows:].reshape(tokens // sections, up.shape[1])

            middle_all = gather_mp(middle)
            partial = times_t(middle_all, weight_last).astype(BF16)
            if section == 0:
                low, up, partial = held(low, up, partial)
            summed = scatter_sum_dp(partial)
            grad = (summed * scales_low[section]).astype(BF16)
            grads[section] = grad
            if section > 0:
                gathered = gather_dp(grad)

    with jax.named_scope("outputs"):
        low = gather_mp(low)

        def columns(array, section):
            turn = last - section
            left = 1 + turn
            right = 0 if turn == 0 else sections + turn
            return [
                array[:, left * rank : (left + 1) * rank],
                array[:, right * rank : (right + 1) * rank],
            ]

        pair = [
            jnp.concatenate(columns(low, s) + columns(up, s), axis=1)
            for s in range(sections)
        ]
        mine = jnp.where(core == 0, pair[0], pair[1])
        other = jnp.where(core == 0, pair[1], pair[0])
        other, grads[0] = held(other, grads[0])
        got = swap_sections(other)

        def joined(own, received, rows):
            own = own.reshape(-1, rows, own.shape[1])
            received = received.reshape(-1, rows, received.shape[1])
            stack = jnp.stack(
                [
                    jnp.where(core == 0, own, received),
                    jnp.where(core == 0, received, own),
                ],
                axis=1,
            )
            return stack.reshape(-1, own.shape[2])

        factors = joined(mine, got, half)
        mine = jnp.where(core == 0, grads[0], grads[1])
        other = jnp.where(core == 0, grads[1], grads[0])
        grads_out = joined(mine, swap_sections(other), half)

        windows = window_slot.shape[0]
        owned = windows // (dp_count * mp_count)
        position = lax.axis_index("dp") * mp_count + lax.axis_index("mp")
        rows = position * owned + jnp.arange(owned, dtype=jnp.int32)
        holds = window_slot[None, :] == rows[:, None]
        window = jnp.sum(
            jnp.where(holds, jnp.arange(windows, dtype=jnp.int32)[None, :], 0), axis=1
        )
        hits = window_ids[None, :] == window[:, None]
        sketches = []
        for place in range(2):
            pair = factors[:, 2 * rank * place : 2 * rank * (place + 1)]
            left = pair[:, :rank]
            right = pair[:, rank:]
            masked = jnp.where(hits[:, :, None], left[None], jnp.zeros((), BF16))
            sums = lax.dot_general(
                masked, right, (((1,), (0,)), ((), ())), preferred_element_type=F32
            )
            sketches.append(sums.reshape(owned, rank * rank))
        sketch = jnp.stack(sketches)
    return (grads_out[None], sketch[None])


def solution(mesh):
    placed = (
        P("dp", "mp"),
        P("section", "dp", "mp"),
        P("section", "mp", "dp"),
        P("section", None, "mp"),
        P("section", None, "dp"),
        P("section", "mp", "dp"),
        P("section", "dp", "mp"),
        P("section", None, "mp"),
        P("section", None, "mp"),
        P("section", None, "dp"),
        P("section", None, "dp"),
        P(),
        P(),
    )
    return jax.shard_map(
        body,
        mesh=mesh,
        in_specs=placed,
        out_specs=(P("section", "dp", "mp"), P("section", None, ("dp", "mp"), None)),
        check_vma=False,
    )
```

```python
import jax
import jax.numpy as jnp
from jax import lax
from jax.sharding import PartitionSpec as P

BF16 = jnp.bfloat16
F32 = jnp.float32


def times_t(left, right):
    return lax.dot_general(
        left, right, (((1,), (1,)), ((), ())), preferred_element_type=F32
    )


def swap_sections(block):
    return lax.ppermute(block, "section", [(0, 1), (1, 0)])


def shift_mp(block, distance):
    count = lax.axis_size("mp")
    return lax.ppermute(
        block, "mp", [(i, (i + distance) % count) for i in range(count)]
    )


def gather_dp(block):
    count = lax.axis_size("dp")
    copies = jnp.broadcast_to(block[None], (count,) + block.shape)
    got = lax.all_to_all(copies, "dp", 0, 0, tiled=True)
    return got.reshape(count * block.shape[0], block.shape[1])


def scatter_sum_dp(partial):
    count = lax.axis_size("dp")
    got = lax.all_to_all(partial, "dp", 0, 0, tiled=True)
    got = got.reshape(count, partial.shape[0] // count, partial.shape[1])
    return jnp.sum(got.astype(F32), axis=0)


def from_all_mp(block):
    count = lax.axis_size("mp")
    return [block] + [shift_mp(block, distance) for distance in range(1, count)]


def scatter_sum_mp(partial):
    count = lax.axis_size("mp")
    mine = lax.axis_index("mp")
    rows = partial.shape[0] // count

    def part(distance):
        return lax.dynamic_slice_in_dim(
            partial, ((mine + distance) % count) * rows, rows, 0
        )

    total = part(0).astype(F32)
    for distance in range(1, count):
        total = total + shift_mp(part(distance), distance).astype(F32)
    return total


def gather_mp(block):
    return in_order(from_all_mp(block))


def in_order(blocks):
    count = lax.axis_size("mp")
    mine = lax.axis_index("mp")
    rows, width = blocks[0].shape
    whole = jnp.zeros((count * rows, width), blocks[0].dtype)
    for distance, got in enumerate(blocks):
        whole = lax.dynamic_update_slice_in_dim(
            whole, got, ((mine - distance) % count) * rows, 0
        )
    return whole


def body(
    out_grad,
    upper_w,
    lower_w,
    upper_in,
    lower_in,
    upper_deriv,
    lower_deriv,
    proj_upper_in,
    proj_upper_out,
    proj_lower_in,
    proj_lower_out,
    window_ids,
    window_slot,
):
    sections = lax.axis_size("section")
    dp_count = lax.axis_size("dp")
    mp_count = lax.axis_size("mp")
    core = lax.axis_index("section")
    rank = proj_upper_in.shape[1]
    tokens_dp, width = out_grad.shape
    hidden = upper_deriv.shape[2]
    tokens = tokens_dp * dp_count
    half = tokens_dp // sections

    def halves(array):
        cut = array.reshape(
            array.shape[0] // tokens_dp, sections, half, array.shape[1]
        )
        mine = lax.dynamic_index_in_dim(cut, core, 1, keepdims=False)
        other = lax.dynamic_index_in_dim(cut, 1 - core, 1, keepdims=False)
        shape = (array.shape[0] // sections, array.shape[1])
        return mine.reshape(shape), other.reshape(shape)

    def swapped(*arrays):
        got = swap_sections(jnp.concatenate(arrays, axis=0))
        cuts = []
        for array in arrays[:-1]:
            cuts.append((cuts[-1] if cuts else 0) + array.shape[0])
        return jnp.split(got, cuts, axis=0)

    def of_section(pair, section):
        own, received = pair
        return jnp.where(core == section, own, received)

    def held(*arrays):
        return lax.optimization_barrier(arrays)

    dp_index = lax.axis_index("dp")
    mp_index = lax.axis_index("mp")
    tokens_mp = upper_deriv.shape[1]

    grad = jnp.where(core == 0, out_grad[:half], out_grad[half:])
    gathered = gather_dp(grad)

    deriv_up, deriv_up_sent = halves(upper_deriv[0])
    deriv_low, deriv_low_sent = halves(lower_deriv[0])
    left_up, left_up_sent = halves(
        times_t(
            lax.dynamic_slice_in_dim(upper_in[0], dp_index * tokens_dp, tokens_dp, 0),
            proj_upper_in[0],
        ).astype(BF16)
    )
    left_low, left_low_sent = halves(
        times_t(
            lax.dynamic_slice_in_dim(lower_in[0], mp_index * tokens_mp, tokens_mp, 0),
            proj_lower_in[0],
        ).astype(BF16)
    )
    weight_up = (upper_w[0], swap_sections(upper_w[0]))
    got = swapped(proj_upper_out[0], deriv_low_sent)
    pout_up = (proj_upper_out[0], got[0])
    deriv_low = (deriv_low, got[1])
    got = swapped(left_up_sent, left_low_sent)
    left_up = (left_up, got[0])
    left_low = (left_low, got[1])
    got = swapped(proj_lower_out[0], deriv_up_sent)
    pout_low = (proj_lower_out[0], got[0])
    deriv_up = (deriv_up, got[1])
    weight_low = (lower_w[0], swap_sections(lower_w[0]))

    last = sections - 1
    pouts_low = held(*[of_section(pout_low, s) for s in range(sections)])
    scales_low = held(*[of_section(deriv_low, s).astype(F32) for s in range(sections)])
    grads = [None] * sections
    ups = []
    lows = []
    for section in range(last, -1, -1):
        with jax.named_scope(f"up_{section}"):
            ups.append(times_t(grad, of_section(pout_up, section)).astype(BF16))
            if section == last:
                ups += [of_section(left_up, s) for s in range(last, -1, -1)]
            if section == 0:
                up = from_all_mp(jnp.concatenate(ups, axis=1))
                up = sum(part.astype(F32) for part in up).astype(BF16)
            weight = of_section(weight_up, section)
            weight_last = of_section(weight_low, section)
            if section == last:
                weight, weight_last, gathered = held(weight, weight_last, gathered)
            summed = scatter_sum_mp(times_t(gathered, weight).astype(BF16))
            scale = of_section(deriv_up, section).astype(F32)
            middle = (summed * scale).astype(BF16)
        with jax.named_scope(f"low_{section}"):
            low = [times_t(middle, pouts_low[section]).astype(BF16)]
            if section == last:
                low += [of_section(left_low, s) for s in range(last, -1, -1)]
            lows += low
            if section == 0:
                low = jnp.concatenate(lows, axis=1)
                rows = low.shape[0]
                both = gather_dp(jnp.concatenate([low, up], axis=0))
                both = both.reshape(dp_count, rows + up.shape[0], up.shape[1])
                low = jnp.sum(both[:, :rows].astype(F32), axis=0).astype(BF16)
                up = both[:, rows:].reshape(tokens // sections, up.shape[1])

            middle_all = gather_mp(middle)
            partial = times_t(middle_all, weight_last).astype(BF16)
            if section == 0:
                low, up, partial = held(low, up, partial)
            summed = scatter_sum_dp(partial)
            grad = (summed * scales_low[section]).astype(BF16)
            grads[section] = grad
            if section > 0:
                gathered = gather_dp(grad)

    with jax.named_scope("outputs"):
        *blocks, grads[0] = held(*from_all_mp(low), grads[0])
        low = in_order(blocks)

        def columns(array, section):
            turn = last - section
            left = 1 + turn
            right = 0 if turn == 0 else sections + turn
            return [
                array[:, left * rank : (left + 1) * rank],
                array[:, right * rank : (right + 1) * rank],
            ]

        pair = [
            jnp.concatenate(columns(low, s) + columns(up, s), axis=1)
            for s in range(sections)
        ]
        mine = jnp.where(core == 0, pair[0], pair[1])
        other = jnp.where(core == 0, pair[1], pair[0])
        got = swap_sections(other)

        def joined(own, received, rows):
            own = own.reshape(-1, rows, own.shape[1])
            received = received.reshape(-1, rows, received.shape[1])
            stack = jnp.stack(
                [
                    jnp.where(core == 0, own, received),
                    jnp.where(core == 0, received, own),
                ],
                axis=1,
            )
            return stack.reshape(-1, own.shape[2])

        factors = joined(mine, got, half)
        mine = jnp.where(core == 0, grads[0], grads[1])
        other = jnp.where(core == 0, grads[1], grads[0])
        grads_out = joined(mine, swap_sections(other), half)

        windows = window_slot.shape[0]
        owned = windows // (dp_count * mp_count)
        position = lax.axis_index("dp") * mp_count + lax.axis_index("mp")
        rows = position * owned + jnp.arange(owned, dtype=jnp.int32)
        holds = window_slot[None, :] == rows[:, None]
        window = jnp.sum(
            jnp.where(holds, jnp.arange(windows, dtype=jnp.int32)[None, :], 0), axis=1
        )
        hits = window_ids[None, :] == window[:, None]
        sketches = []
        for place in range(2):
            pair = factors[:, 2 * rank * place : 2 * rank * (place + 1)]
            left = pair[:, :rank]
            right = pair[:, rank:]
            masked = jnp.where(hits[:, :, None], left[None], jnp.zeros((), BF16))
            sums = lax.dot_general(
                masked, right, (((1,), (0,)), ((), ())), preferred_element_type=F32
            )
            sketches.append(sums.reshape(owned, rank * rank))
        sketch = jnp.stack(sketches)
    return (grads_out[None], sketch[None])


def solution(mesh):
    placed = (
        P("dp", "mp"),
        P("section", "dp", "mp"),
        P("section", "mp", "dp"),
        P("section", None, "mp"),
        P("section", None, "dp"),
        P("section", "mp", "dp"),
        P("section", "dp", "mp"),
        P("section", None, "mp"),
        P("section", None, "mp"),
        P("section", None, "dp"),
        P("section", None, "dp"),
        P(),
        P(),
    )
    return jax.shard_map(
        body,
        mesh=mesh,
        in_specs=placed,
        out_specs=(P("section", "dp", "mp"), P("section", None, ("dp", "mp"), None)),
        check_vma=False,
    )
```

```python
import jax
import jax.numpy as jnp
from jax import lax
from jax.sharding import PartitionSpec as P

BF16 = jnp.bfloat16
F32 = jnp.float32


def times_t(left, right):
    return lax.dot_general(
        left, right, (((1,), (1,)), ((), ())), preferred_element_type=F32
    )


def swap_sections(block):
    return lax.ppermute(block, "section", [(0, 1), (1, 0)])


def shift_mp(block, distance):
    count = lax.axis_size("mp")
    return lax.ppermute(
        block, "mp", [(i, (i + distance) % count) for i in range(count)]
    )


def gather_dp(block):
    count = lax.axis_size("dp")
    copies = jnp.broadcast_to(block[None], (count,) + block.shape)
    got = lax.all_to_all(copies, "dp", 0, 0, tiled=True)
    return got.reshape(count * block.shape[0], block.shape[1])


def scatter_sum_dp(partial):
    count = lax.axis_size("dp")
    got = lax.all_to_all(partial, "dp", 0, 0, tiled=True)
    got = got.reshape(count, partial.shape[0] // count, partial.shape[1])
    return jnp.sum(got.astype(F32), axis=0)


def from_all_mp(block):
    count = lax.axis_size("mp")
    return [block] + [shift_mp(block, distance) for distance in range(1, count)]


def scatter_sum_mp(partial):
    count = lax.axis_size("mp")
    mine = lax.axis_index("mp")
    rows = partial.shape[0] // count

    def part(distance):
        return lax.dynamic_slice_in_dim(
            partial, ((mine + distance) % count) * rows, rows, 0
        )

    total = part(0).astype(F32)
    for distance in range(1, count):
        total = total + shift_mp(part(distance), distance).astype(F32)
    return total


def gather_mp(block):
    got = {distance: shift_mp(block, distance) for distance in (2, 1, 3)}
    return in_order([block] + [got[distance] for distance in range(1, len(got) + 1)])


def in_order(blocks):
    count = lax.axis_size("mp")
    mine = lax.axis_index("mp")
    rows, width = blocks[0].shape
    whole = jnp.zeros((count * rows, width), blocks[0].dtype)
    for distance, got in enumerate(blocks):
        whole = lax.dynamic_update_slice_in_dim(
            whole, got, ((mine - distance) % count) * rows, 0
        )
    return whole


def body(
    out_grad,
    upper_w,
    lower_w,
    upper_in,
    lower_in,
    upper_deriv,
    lower_deriv,
    proj_upper_in,
    proj_upper_out,
    proj_lower_in,
    proj_lower_out,
    window_ids,
    window_slot,
):
    sections = lax.axis_size("section")
    dp_count = lax.axis_size("dp")
    mp_count = lax.axis_size("mp")
    core = lax.axis_index("section")
    rank = proj_upper_in.shape[1]
    tokens_dp, width = out_grad.shape
    hidden = upper_deriv.shape[2]
    tokens = tokens_dp * dp_count
    half = tokens_dp // sections

    def halves(array):
        cut = array.reshape(
            array.shape[0] // tokens_dp, sections, half, array.shape[1]
        )
        mine = lax.dynamic_index_in_dim(cut, core, 1, keepdims=False)
        other = lax.dynamic_index_in_dim(cut, 1 - core, 1, keepdims=False)
        shape = (array.shape[0] // sections, array.shape[1])
        return mine.reshape(shape), other.reshape(shape)

    def swapped(*arrays):
        got = swap_sections(jnp.concatenate(arrays, axis=0))
        cuts = []
        for array in arrays[:-1]:
            cuts.append((cuts[-1] if cuts else 0) + array.shape[0])
        return jnp.split(got, cuts, axis=0)

    def of_section(pair, section):
        own, received = pair
        return jnp.where(core == section, own, received)

    def held(*arrays):
        return lax.optimization_barrier(arrays)

    dp_index = lax.axis_index("dp")
    mp_index = lax.axis_index("mp")
    tokens_mp = upper_deriv.shape[1]

    grad = jnp.where(core == 0, out_grad[:half], out_grad[half:])
    copies = jnp.where(
        core == 0,
        jnp.broadcast_to(out_grad[None, :half], (dp_count, half, width)),
        jnp.broadcast_to(out_grad[None, half:], (dp_count, half, width)),
    )
    gathered = lax.all_to_all(copies, "dp", 0, 0, tiled=True)
    gathered = gathered.reshape(tokens // sections, width)

    deriv_up, deriv_up_sent = halves(upper_deriv[0])
    deriv_low, deriv_low_sent = halves(lower_deriv[0])
    left_up, left_up_sent = halves(
        times_t(
            lax.dynamic_slice_in_dim(upper_in[0], dp_index * tokens_dp, tokens_dp, 0),
            proj_upper_in[0],
        ).astype(BF16)
    )
    left_low, left_low_sent = halves(
        times_t(
            lax.dynamic_slice_in_dim(lower_in[0], mp_index * tokens_mp, tokens_mp, 0),
            proj_lower_in[0],
        ).astype(BF16)
    )
    weight_up = (upper_w[0], swap_sections(upper_w[0]))
    got = swapped(proj_upper_out[0], deriv_low_sent)
    pout_up = (proj_upper_out[0], got[0])
    deriv_low = (deriv_low, got[1])
    got = swapped(left_up_sent, left_low_sent)
    left_up = (left_up, got[0])
    left_low = (left_low, got[1])
    got = swapped(proj_lower_out[0], deriv_up_sent)
    pout_low = (proj_lower_out[0], got[0])
    deriv_up = (deriv_up, got[1])
    weight_low = (lower_w[0], swap_sections(lower_w[0]))

    last = sections - 1
    pouts_low = held(*[of_section(pout_low, s) for s in range(sections)])
    scales_low = held(*[of_section(deriv_low, s).astype(F32) for s in range(sections)])
    grads = [None] * sections
    ups = []
    lows = []
    for section in range(last, -1, -1):
        with jax.named_scope(f"up_{section}"):
            ups.append(times_t(grad, of_section(pout_up, section)).astype(BF16))
            if section == last:
                ups += [of_section(left_up, s) for s in range(last, -1, -1)]
            if section == 0:
                up = from_all_mp(jnp.concatenate(ups, axis=1))
                up = sum(part.astype(F32) for part in up).astype(BF16)
            weight = of_section(weight_up, section)
            weight_last = of_section(weight_low, section)
            if section == last:
                weight, weight_last, gathered = held(weight, weight_last, gathered)
            summed = scatter_sum_mp(times_t(gathered, weight).astype(BF16))
            scale = of_section(deriv_up, section).astype(F32)
            middle = (summed * scale).astype(BF16)
        with jax.named_scope(f"low_{section}"):
            low = [times_t(middle, pouts_low[section]).astype(BF16)]
            if section == last:
                low += [of_section(left_low, s) for s in range(last, -1, -1)]
            lows += low
            if section == 0:
                low = jnp.concatenate(lows, axis=1)
                rows = low.shape[0]
                both = gather_dp(jnp.concatenate([low, up], axis=0))
                both = both.reshape(dp_count, rows + up.shape[0], up.shape[1])
                low = jnp.sum(both[:, :rows].astype(F32), axis=0).astype(BF16)
                up = both[:, rows:].reshape(tokens // sections, up.shape[1])

            middle_all = gather_mp(middle)
            partial = times_t(middle_all, weight_last).astype(BF16)
            if section == 0:
                low, up, partial = held(low, up, partial)
            summed = scatter_sum_dp(partial)
            grad = (summed * scales_low[section]).astype(BF16)
            grads[section] = grad
            if section > 0:
                gathered = gather_dp(grad)

    with jax.named_scope("outputs"):
        def columns(array, section):
            turn = last - section
            left = 1 + turn
            right = 0 if turn == 0 else sections + turn
            return jnp.concatenate(
                [
                    array[:, left * rank : (left + 1) * rank],
                    array[:, right * rank : (right + 1) * rank],
                ],
                axis=1,
            )

        def exchanged_columns(array):
            first, second = columns(array, 0), columns(array, 1)
            mine = jnp.where(core == 0, first, second)
            return mine, swap_sections(jnp.where(core == 0, second, first))

        blocks = from_all_mp(low)
        up_mine, up_got = exchanged_columns(up)
        *blocks, up_got, grads[0] = held(*blocks, up_got, grads[0])
        low_mine, low_got = exchanged_columns(in_order(blocks))

        def joined(own, received, rows):
            own = own.reshape(-1, rows, own.shape[1])
            received = received.reshape(-1, rows, received.shape[1])
            stack = jnp.stack(
                [
                    jnp.where(core == 0, own, received),
                    jnp.where(core == 0, received, own),
                ],
                axis=1,
            )
            return stack.reshape(-1, own.shape[2])

        factors = jnp.concatenate(
            [joined(low_mine, low_got, half), joined(up_mine, up_got, half)], axis=1
        )
        mine = jnp.where(core == 0, grads[0], grads[1])
        other = jnp.where(core == 0, grads[1], grads[0])
        grads_out = joined(mine, swap_sections(other), half)

        windows = window_slot.shape[0]
        owned = windows // (dp_count * mp_count)
        position = lax.axis_index("dp") * mp_count + lax.axis_index("mp")
        rows = position * owned + jnp.arange(owned, dtype=jnp.int32)
        holds = window_slot[None, :] == rows[:, None]
        window = jnp.sum(
            jnp.where(holds, jnp.arange(windows, dtype=jnp.int32)[None, :], 0), axis=1
        )
        hits = window_ids[None, :] == window[:, None]
        sketches = []
        for place in range(2):
            pair = factors[:, 2 * rank * place : 2 * rank * (place + 1)]
            left = pair[:, :rank]
            right = pair[:, rank:]
            masked = jnp.where(hits[:, :, None], left[None], jnp.zeros((), BF16))
            sums = lax.dot_general(
                masked, right, (((1,), (0,)), ((), ())), preferred_element_type=F32
            )
            sketches.append(sums.reshape(owned, rank * rank))
        sketch = jnp.stack(sketches)
    return (grads_out[None], sketch[None])


def solution(mesh):
    placed = (
        P("dp", "mp"),
        P("section", "dp", "mp"),
        P("section", "mp", "dp"),
        P("section", None, "mp"),
        P("section", None, "dp"),
        P("section", "mp", "dp"),
        P("section", "dp", "mp"),
        P("section", None, "mp"),
        P("section", None, "mp"),
        P("section", None, "dp"),
        P("section", None, "dp"),
        P(),
        P(),
    )
    return jax.shard_map(
        body,
        mesh=mesh,
        in_specs=placed,
        out_specs=(P("section", "dp", "mp"), P("section", None, ("dp", "mp"), None)),
        check_vma=False,
    )
```
